32 devices in a mesh: groups: 2 (over y), row: 8 (over z, x), col: 2 (over core).
Axes of the slice: x: 2, y: 2, z: 4, core: 2. Of those that a mesh axis runs over, the one named last changes fastest.
Arguments:
- inputs: bfloat16 [32, 8192], P(('groups', 'row'), 'col'), parts along dimension 0, may hold values from -6 to 6
- out_grads: bfloat16 [32, 8192], P(('groups', 'row'), 'col'), parts along dimension 0, may hold values from -6 to 6
- w_gate: bfloat16 [8192, 24576], P('col', 'row'), may hold values from -0.0625 to 0.0625
- w_up: bfloat16 [8192, 24576], P('col', 'row'), may hold values from -0.0625 to 0.0625
- w_down: bfloat16 [24576, 8192], P('row', 'col'), may hold values from -0.0390625 to 0.0390625
Outputs:
- attribution: float32 [32, 8192], P(('groups', 'row'), 'col'), parts along dimension 0
The draws below stay inside these ranges and needn't reach their ends.
There are 2 independent parts, one for each index of `groups`. The reference program is written for one: setup_inputs(seed, part) draws one part's arguments, and reference() takes and returns one part's arrays. A program takes and returns all parts, laid end to end along the dimension named above; an argument that names none is the same for every part. Nothing has to cross between parts.
All inputs are finite; a program needn't handle non-finite values.
Results may differ from the reference program's by a relative error of at most 0.0029.
Values may be sent and summed in bfloat16 or wider, within the bound.
A program may use at most 192 MiB of HBM per device.

```python
import jax
import jax.numpy as jnp
from jax import lax

D = 8192
FF = 24576
TOKENS = 16


def levels(own_key, extent, shards, low, high):
    factor_of = 1.0
    for axis_at, parts in shards:
        draws = jax.random.uniform(jax.random.fold_in(jax.random.fold_in(own_key, 6), axis_at), (parts,), jnp.float32, low / len(shards), high / len(shards))
        factor_of = factor_of * jnp.repeat(jnp.exp(draws), extent[axis_at] // parts).reshape((-1,) + (1,) * (len(extent) - 1 - axis_at))
    return factor_of


def centred(key, shape, width, limit, split=(), dtype=jnp.bfloat16):
    level = levels(key, shape, split, -0.22, 0.18) if split else 1.0
    array = jax.random.normal(key, shape, jnp.float32) * width * level
    return jnp.minimum(jnp.maximum(array, -limit), limit).astype(dtype)


def setup_inputs(seed: int = 0, part: int = 0) -> dict:
    splits = jax.random.split(jax.random.key(seed), 6)
    part_keys = jax.random.split(jax.random.fold_in(splits[5], part), 6)
    inputs = centred(part_keys[0], (TOKENS, D), 1.0, 6.0, ((0, 8), (1, 2)))
    out_grads = centred(part_keys[1], (TOKENS, D), 1.0, 6.0, ((0, 8), (1, 2)))
    w_gate = centred(splits[2], (D, FF), D ** -0.5, 0.0625, ((0, 2), (1, 8)))
    w_up = centred(splits[3], (D, FF), D ** -0.5, 0.0625, ((0, 2), (1, 8)))
    w_down = centred(splits[4], (FF, D), FF ** -0.5, 0.0390625, ((0, 8), (1, 2)))
    return dict(inputs=inputs, out_grads=out_grads, w_gate=w_gate, w_up=w_up, w_down=w_down)


def reference(inputs, out_grads, w_gate, w_up, w_down):
    gated = jnp.dot(inputs, w_gate, preferred_element_type=jnp.float32)
    upward = jnp.dot(inputs, w_up, preferred_element_type=jnp.float32)
    backward = lax.dot_general(out_grads, w_down, (((1,), (1,)), ((), ())), preferred_element_type=jnp.float32)
    sigma = jax.nn.sigmoid(gated)
    grad_gate = (backward * upward * sigma * (1.0 + gated * (1.0 - sigma))).astype(jnp.bfloat16)
    grad_up = (backward * gated * sigma).astype(jnp.bfloat16)
    grad_input = lax.dot_general(grad_gate, w_gate, (((1,), (1,)), ((), ())), preferred_element_type=jnp.float32)
    grad_input = grad_input + lax.dot_general(grad_up, w_up, (((1,), (1,)), ((), ())), preferred_element_type=jnp.float32)
    return inputs.astype(jnp.float32) * grad_input
```

```python
import functools

import jax
import jax.numpy as jnp
from jax import lax
from jax.experimental import pallas as pl
from jax.experimental.pallas import tpu as pltpu
from jax.sharding import PartitionSpec as P

MESH = pl.DeviceIdType.MESH
TILE = 512
CHUNKS = 2
PADDED = 128
LEAD = 12
NT = (((1,), (1,)), ((), ()))


def derivatives(sums):
    gated = sums[0]
    upward = sums[1]
    backward = sums[2]
    sigma = jax.nn.sigmoid(gated)
    grad_gate = (backward * upward * sigma * (1.0 + gated * (1.0 - sigma))).astype(jnp.bfloat16)
    grad_up = (backward * gated * sigma).astype(jnp.bfloat16)
    return jnp.stack([grad_gate, grad_up])


def per_device(inputs, out_grads, w_gate, w_up, w_down):
    stacked = jnp.stack([inputs, out_grads])
    piece = lax.all_gather(stacked, "row", axis=1, tiled=True)
    gated = jnp.dot(piece[0], w_gate, preferred_element_type=jnp.float32)
    upward = jnp.dot(piece[0], w_up, preferred_element_type=jnp.float32)
    backward = lax.dot_general(piece[1], w_down, NT, preferred_element_type=jnp.float32)
    partial_sums = jnp.stack([gated, upward, backward])
    summed = lax.psum(partial_sums, "col")
    derived = derivatives(summed)
    total = lax.dot_general(derived[0], w_gate, NT, preferred_element_type=jnp.float32)
    grad_input = lax.psum_scatter(
        total + lax.dot_general(derived[1], w_up, NT, preferred_element_type=jnp.float32),
        "row",
        scatter_dimension=0,
        tiled=True,
    )
    return inputs.astype(jnp.float32) * grad_input


def kernel(
    nz, nf, nh,
    in_hbm, og_hbm, wg_hbm, wu_hbm, wd_hbm, out_ref,
    wa, wb, dt, gt, gx, gy, stage, xs, ys, part, peer, dg, du, acc, s0, r0,
    w_sem, l_sem, z_send, z_recv, p_send, p_recv, c_send, c_recv, r_send, r_recv,
):
    tokens, feats = in_hbm.shape
    rows = nz * tokens
    every = 4 * rows
    half = nh * TILE
    blocks = nf * nh
    width = feats // CHUNKS
    per = width // TILE
    g = lax.axis_index("groups")
    r = lax.axis_index("row")
    c = lax.axis_index("col")
    x = lax.rem(r, 2)
    z = r // 2
    plane = g * 2 + x

    def p_index(d):
        return lax.rem(plane + d, 4)

    def device(dz, dp):
        q = lax.rem(plane + dp, 4)
        return {"groups": q // 2, "row": lax.rem(z + dz, nz) * 2 + lax.rem(q, 2)}

    hops = [(dz, dp) for dz in (2, 1, 3, 0) for dp in range(4)]
    hops = [(dz, dp) for dz, dp in hops if dz < nz and (dz or dp)]
    hops += [(dz, dp) for dz in range(4, nz) for dp in range(4)]

    def remote(src, dst, send, recv, to):
        return pltpu.make_async_remote_copy(
            src_ref=src, dst_ref=dst, send_sem=send, recv_sem=recv,
            device_id=to, device_id_type=MESH,
        )

    def hid(b):
        return pl.ds(pl.multiple_of(g * half + (b // nf) * TILE, TILE), TILE)

    def fea(b):
        return pl.ds(pl.multiple_of(lax.rem(b, nf) * TILE, TILE), TILE)

    def load_down(b):
        return pltpu.make_async_copy(wd_hbm.at[hid(b), fea(b)], wa.at[b], w_sem.at[0, b])

    def load_gate(b):
        return pltpu.make_async_copy(wg_hbm.at[fea(b), hid(b)], wb.at[b], w_sem.at[1, b])

    def load_up(b):
        return pltpu.make_async_copy(wu_hbm.at[fea(b), hid(b)], wa.at[b], w_sem.at[2, b])

    own = [
        pltpu.make_async_copy(in_hbm, gx.at[plane, z], l_sem.at[0]),
        pltpu.make_async_copy(og_hbm, gy.at[plane, z], l_sem.at[1]),
    ]
    for copy in own:
        copy.start()

    barrier = pltpu.get_barrier_semaphore()
    for dz, dp in hops:
        pl.semaphore_signal(barrier, inc=1, device_id=device(dz, dp), device_id_type=MESH)
    pl.semaphore_signal(barrier, inc=1, device_id={"col": 1 - c}, device_id_type=MESH)

    @pl.loop(0, blocks)
    def _(b):
        load_down(b).start()

    xs[...] = jnp.zeros_like(xs)
    ys[...] = jnp.zeros_like(ys)
    dg[...] = jnp.zeros_like(dg)
    du[...] = jnp.zeros_like(du)

    def turn_down(b):
        load_down(b).wait()
        dt[b] = wa[b].T
        load_gate(b).start()
        load_up(b).start()

    early = blocks - z * (blocks // nz + 2)
    early = lax.max(early, 0)
    pl.loop(0, early)(turn_down)

    pl.semaphore_wait(barrier, len(hops) + 1)

    sources = ((in_hbm, gx), (og_hbm, gy))
    z_copies = [
        [
            remote(src, buf.at[plane, z], z_send.at[a, d - 1], z_recv.at[a, d - 1], device(d, 0))
            for d in range(1, nz)
        ]
        for a, (src, buf) in enumerate(sources)
    ]
    p_copies = []
    for a, (src, buf) in enumerate(sources):
        p_copies.append([])
        for k in range(nz):
            block = buf.at[plane, lax.rem(z + nz - k, nz)]
            p_copies[a].append([
                remote(block if k else src, block, p_send.at[a, k, d - 1], p_recv.at[a, k, d - 1], device(0, d))
                for d in range(1, 4)
            ])

    def relay(a):
        for k in range(1, nz):
            z_copies[a][k - 1].wait_recv()
            for copy in p_copies[a][k]:
                copy.start()

    for copy in z_copies[0] + p_copies[0][0] + z_copies[1]:
        copy.start()

    pl.loop(early, blocks)(turn_down)

    def turn_gate(b):
        load_gate(b).wait()
        gt[b] = wb[b].T

    relay(0)
    pl.loop(0, LEAD)(turn_gate)
    for copy in p_copies[1][0]:
        copy.start()
    relay(1)
    pl.loop(LEAD, blocks)(turn_gate)

    def arrange(a, buf, dst):
        own[a].wait()
        for copies in p_copies[a]:
            for copy in copies:
                copy.wait_recv()
        for q in range(4):
            for k in range(nz):
                at = q * rows + k * tokens
                stage[at:at + tokens, :] = buf[q, k].astype(jnp.float32)
        dst[0:every, :] = stage[...].astype(jnp.bfloat16)

    other = {"col": 1 - c}
    moves = [
        [remote(part.at[m, j], peer.at[m, j], c_send.at[m, j], c_recv.at[m, j], other) for j in range(nh)]
        for m in range(3)
    ]

    def forward(m, j, lhs, weights, turn):
        total = jnp.zeros((every, TILE), jnp.float32)
        for f in range(nf):
            b = j * nf + f
            if turn(b):
                wb[b] = wa[b].T
            total += jnp.dot(
                lhs[:, f * TILE:(f + 1) * TILE], weights[b], preferred_element_type=jnp.float32
            )[0:every]
        part[m, j] = total
        moves[m][j].start()

    arrange(0, gx, xs)
    for j in range(nh):
        forward(0, j, xs, wb, lambda b: False)
    cut = nh // 2 * nf + nf // 2
    for b in range(blocks):
        load_up(b).wait()
    for j in range(nh):
        forward(1, j, xs, wa, lambda b: b < cut)
    arrange(1, gy, ys)
    for j in range(nh):
        forward(2, j, ys, dt, lambda b: b >= cut)

    def derive(j):
        for m in range(3):
            moves[m][j].wait_recv()
        gated = part[0, j] + peer[0, j]
        upward = part[1, j] + peer[1, j]
        backward = part[2, j] + peer[2, j]
        sigma = 1.0 / (1.0 + jnp.exp(-gated))
        cols = slice(j * TILE, (j + 1) * TILE)
        dg[0:every, cols] = (backward * upward * sigma * (1.0 + gated * (1.0 - sigma))).astype(jnp.bfloat16)
        du[0:every, cols] = (backward * gated * sigma).astype(jnp.bfloat16)

    def product(f, lo, hi):
        total = jnp.zeros((every, TILE), jnp.float32)
        for j in range(lo, hi):
            cols = slice(j * TILE, (j + 1) * TILE)
            b = j * nf + f
            total += jnp.dot(dg[:, cols], gt[b], preferred_element_type=jnp.float32)[0:every]
            total += jnp.dot(du[:, cols], wb[b], preferred_element_type=jnp.float32)[0:every]
        return total

    sums = [
        [
            remote(
                s0.at[n, p_index(dp), lax.rem(z + dz, nz)], r0.at[n, i],
                r_send.at[n, i], r_recv.at[n, i], device(dz, dp),
            )
            for i, (dz, dp) in enumerate(hops)
        ]
        for n in range(CHUNKS)
    ]

    def send(n):
        at = slice(n * width, (n + 1) * width)
        for q in range(4):
            for k in range(nz):
                top = q * rows + k * tokens
                s0[n, q, k] = acc[top:top + tokens, at].astype(jnp.bfloat16)
        for copy in sums[n]:
            copy.start()

    def store(n):
        at = slice(n * width, (n + 1) * width)
        total = s0[n, plane, z].astype(jnp.float32)
        for i in range(len(hops)):
            sums[n][i].wait_recv()
            total = total + r0[n, i].astype(jnp.float32)
        out_ref[:, at] = gx[plane, z, :, at].astype(jnp.float32) * total

    def columns(f):
        return slice(f * TILE, (f + 1) * TILE)

    for j in range(nh - 1):
        derive(j)
    for f in range(per):
        acc[:, columns(f)] = product(f, 0, nh - 1)
    derive(nh - 1)
    for f in range(per):
        acc[:, columns(f)] += product(f, nh - 1, nh)
    send(0)
    for n in range(1, CHUNKS):
        for f in range(n * per, (n + 1) * per):
            acc[:, columns(f)] = product(f, 0, nh)
        send(n)
    for n in range(CHUNKS):
        store(n)

    for copies in z_copies + p_copies[0] + p_copies[1] + moves + sums:
        for copy in copies:
            copy.wait_send()


def shared(nz, inputs, out_grads, w_gate, w_up, w_down):
    tokens, feats = inputs.shape
    half = w_gate.shape[1] // 2
    nh = half // TILE
    nf = feats // TILE
    width = feats // CHUNKS
    rows = nz * tokens
    every = 4 * rows
    others = 4 * nz - 1
    f32, bf16 = jnp.float32, jnp.bfloat16
    dma = pltpu.SemaphoreType.DMA
    return pl.pallas_call(
        functools.partial(kernel, nz, nf, nh),
        out_shape=jax.ShapeDtypeStruct((tokens, feats), f32),
        in_specs=[pl.BlockSpec(memory_space=pl.ANY)] * 5,
        out_specs=pl.BlockSpec(memory_space=pltpu.VMEM),
        scratch_shapes=[
            pltpu.VMEM((nf * nh, TILE, TILE), bf16),
            pltpu.VMEM((nf * nh, TILE, TILE), bf16),
            pltpu.VMEM((nf * nh, TILE, TILE), bf16),
            pltpu.VMEM((nf * nh, TILE, TILE), bf16),
            pltpu.VMEM((4, nz, tokens, feats), bf16),
            pltpu.VMEM((4, nz, tokens, feats), bf16),
            pltpu.VMEM((every, feats), f32),
            pltpu.VMEM((PADDED, feats), bf16),
            pltpu.VMEM((PADDED, feats), bf16),
            pltpu.VMEM((3, nh, every, TILE), f32),
            pltpu.VMEM((3, nh, every, TILE), f32),
            pltpu.VMEM((PADDED, half), bf16),
            pltpu.VMEM((PADDED, half), bf16),
            pltpu.VMEM((every, feats), f32),
            pltpu.VMEM((CHUNKS, 4, nz, tokens, width), bf16),
            pltpu.VMEM((CHUNKS, others, tokens, width), bf16),
            dma((3, nf * nh)), dma((2,)),
            dma((2, nz - 1)), dma((2, nz - 1)),
            dma((2, nz, 3)), dma((2, nz, 3)),
            dma((3, nh)), dma((3, nh)),
            dma((CHUNKS, others)), dma((CHUNKS, others)),
        ],
        compiler_params=pltpu.CompilerParams(
            collective_id=0, has_side_effects=True, vmem_limit_bytes=60 << 20
        ),
    )(inputs, out_grads, w_gate, w_up, w_down)


def solution(mesh):
    in_specs = (
        P(("groups", "row"), "col"),
        P(("groups", "row"), "col"),
        P("col", "row"),
        P("col", "row"),
        P("row", "col"),
    )
    out_specs = P(("groups", "row"), "col")
    groups, row, col = (mesh.shape[name] for name in ("groups", "row", "col"))

    def body(inputs, out_grads, w_gate, w_up, w_down):
        tokens, feats = inputs.shape
        nz = row // 2
        hidden = w_gate.shape[1]
        held = 4 * feats * hidden + 70 * groups * row * tokens * feats
        fits = (
            groups == 2 and col == 2 and row % 2 == 0 and nz > 1
            and hidden % (2 * TILE) == 0 and feats % (TILE * CHUNKS) == 0 and hidden > 2 * TILE
            and nz * tokens == 8 and held < (58 << 20)
        )
        plan = functools.partial(shared, nz) if fits else per_device
        return plan(inputs, out_grads, w_gate, w_up, w_down)

    return jax.shard_map(
        body, mesh=mesh, in_specs=in_specs, out_specs=out_specs, check_vma=False
    )
```

```python
import functools

import jax
import jax.numpy as jnp
from jax import lax
from jax.experimental import pallas as pl
from jax.experimental.pallas import tpu as pltpu
from jax.sharding import PartitionSpec as P

MESH = pl.DeviceIdType.MESH
TILE = 512
CHUNKS = 2
PADDED = 128
FIRST, STEP, SECOND, THIRD = 8, 2, 20, 8
SLOT = (0, 1, 2)
NT = (((1,), (1,)), ((), ()))


def derivatives(sums):
    gated = sums[0]
    upward = sums[1]
    backward = sums[2]
    sigma = jax.nn.sigmoid(gated)
    grad_gate = (backward * upward * sigma * (1.0 + gated * (1.0 - sigma))).astype(jnp.bfloat16)
    grad_up = (backward * gated * sigma).astype(jnp.bfloat16)
    return jnp.stack([grad_gate, grad_up])


def per_device(inputs, out_grads, w_gate, w_up, w_down):
    stacked = jnp.stack([inputs, out_grads])
    piece = lax.all_gather(stacked, "row", axis=1, tiled=True)
    gated = jnp.dot(piece[0], w_gate, preferred_element_type=jnp.float32)
    upward = jnp.dot(piece[0], w_up, preferred_element_type=jnp.float32)
    backward = lax.dot_general(piece[1], w_down, NT, preferred_element_type=jnp.float32)
    partial_sums = jnp.stack([gated, upward, backward])
    summed = lax.psum(partial_sums, "col")
    derived = derivatives(summed)
    total = lax.dot_general(derived[0], w_gate, NT, preferred_element_type=jnp.float32)
    grad_input = lax.psum_scatter(
        total + lax.dot_general(derived[1], w_up, NT, preferred_element_type=jnp.float32),
        "row",
        scatter_dimension=0,
        tiled=True,
    )
    return inputs.astype(jnp.float32) * grad_input


def kernel(
    nz, nf, nh,
    in_hbm, og_hbm, wg_hbm, wu_hbm, wd_hbm, out_ref,
    wa, wb, dt, gt, gx, gy, stage, xs, ys, part, peer, dg, du, acc, s0, r0,
    w_sem, l_sem, z_send, z_recv, p_send, p_recv, c_send, c_recv, r_send, r_recv,
):
    tokens, feats = in_hbm.shape
    rows = nz * tokens
    every = 4 * rows
    half = nh * TILE
    blocks = nf * nh
    width = feats // CHUNKS
    per = width // TILE
    g = lax.axis_index("groups")
    r = lax.axis_index("row")
    c = lax.axis_index("col")
    x = lax.rem(r, 2)
    z = r // 2
    plane = g * 2 + x

    def p_index(d):
        return lax.rem(plane + d, 4)

    def device(dz, dp):
        q = lax.rem(plane + dp, 4)
        return {"groups": q // 2, "row": lax.rem(z + dz, nz) * 2 + lax.rem(q, 2)}

    hops = [(dz, dp) for dz in (2, 1, 3, 0) for dp in range(4)]
    hops = [(dz, dp) for dz, dp in hops if dz < nz and (dz or dp)]
    hops += [(dz, dp) for dz in range(4, nz) for dp in range(4)]

    def remote(src, dst, send, recv, to):
        return pltpu.make_async_remote_copy(
            src_ref=src, dst_ref=dst, send_sem=send, recv_sem=recv,
            device_id=to, device_id_type=MESH,
        )

    def hid(b):
        return pl.ds(pl.multiple_of(g * half + (b // nf) * TILE, TILE), TILE)

    def fea(b):
        return pl.ds(pl.multiple_of(lax.rem(b, nf) * TILE, TILE), TILE)

    def load_down(b):
        return pltpu.make_async_copy(wd_hbm.at[hid(b), fea(b)], wa.at[b], w_sem.at[0, b])

    def load_gate(b):
        return pltpu.make_async_copy(wg_hbm.at[fea(b), hid(b)], wb.at[b], w_sem.at[1, b])

    def load_up(b):
        return pltpu.make_async_copy(wu_hbm.at[fea(b), hid(b)], wa.at[b], w_sem.at[2, b])

    own = [
        pltpu.make_async_copy(in_hbm, gx.at[plane, z], l_sem.at[0]),
        pltpu.make_async_copy(og_hbm, gy.at[plane, z], l_sem.at[1]),
    ]
    for copy in own:
        copy.start()

    barrier = pltpu.get_barrier_semaphore()
    for dz, dp in [h for h in hops if 0 in h]:
        pl.semaphore_signal(barrier, inc=1, device_id=device(dz, dp), device_id_type=MESH)
    pl.semaphore_signal(barrier, inc=1, device_id={"col": 1 - c}, device_id_type=MESH)

    @pl.loop(0, blocks)
    def _(b):
        load_down(b).start()

    @pl.loop(0, blocks)
    def _(b):
        load_gate(b).start()

    xs[...] = jnp.zeros_like(xs)
    ys[...] = jnp.zeros_like(ys)
    dg[...] = jnp.zeros_like(dg)
    du[...] = jnp.zeros_like(du)

    def turn_down(b):
        load_down(b).wait()
        dt[b] = wa[b].T
        load_up(b).start()

    for copy in own:
        copy.wait()

    def turn_gate(b):
        load_gate(b).wait()
        gt[b] = wb[b].T

    def turn(lo, hi):
        lo, hi = lax.min(lo, 2 * blocks), lax.min(hi, 2 * blocks)
        pl.loop(lax.min(lo, blocks), lax.min(hi, blocks))(turn_down)
        pl.loop(lax.max(lo - blocks, 0), lax.max(hi - blocks, 0))(turn_gate)

    early = lax.max(FIRST - z * STEP, 0)
    turn(jnp.int32(0), early)

    pl.semaphore_wait(barrier, nz + 3)

    buffers = (gx, gy)

    def source(k):
        if k == 0:
            return z
        return jnp.where(z >= k, z - k, k)

    z_copies = [
        [
            remote(buf.at[plane, z], buf.at[plane, z], z_send.at[a, d - 1], z_recv.at[a, d - 1], device(d, 0))
            for d in range(1, nz)
        ]
        for a, buf in enumerate(buffers)
    ]
    p_copies = []
    for a, buf in enumerate(buffers):
        p_copies.append([])
        for k in range(nz):
            block = buf.at[plane, source(k)]
            p_copies[a].append([
                remote(block, block, p_send.at[a, k, d - 1], p_recv.at[a, k, d - 1], device(0, d))
                for d in range(1, 4)
            ])

    def relay(a):
        for k in range(1, nz):
            shift = lax.rem(z + nz - source(k), nz)
            remote(
                buffers[a].at[plane, source(k)], buffers[a].at[plane, source(k)],
                z_send.at[a, shift - 1], z_recv.at[a, shift - 1], device(1, 0),
            ).wait_recv()
            for copy in p_copies[a][k]:
                copy.start()

    for copy in z_copies[0] + p_copies[0][0] + z_copies[1]:
        copy.start()

    turn(early, early + SECOND)
    relay(0)
    turn(early + SECOND, early + SECOND + THIRD)
    for copy in p_copies[1][0]:
        copy.start()
    relay(1)
    turn(early + SECOND + THIRD, jnp.int32(2 * blocks))

    def arrange(a, buf, dst):
        for copies in p_copies[a]:
            for copy in copies:
                copy.wait_recv()
        for q in range(4):
            for k in range(nz):
                at = q * rows + k * tokens
                stage[at:at + tokens, :] = buf[q, k].astype(jnp.float32)
        dst[0:every, :] = stage[...].astype(jnp.bfloat16)

    other = {"col": 1 - c}
    moves = [
        [remote(part.at[m, j], peer.at[m, j], c_send.at[m, j], c_recv.at[m, j], other) for j in range(nh)]
        for m in range(3)
    ]

    turns = [[] for _ in range(3 * nh)]
    slots = 3 * nh - 1
    for b in range(blocks):
        turns[max(1 + b * slots // blocks, b // nf + 1)].append(b)

    def forward(m, j, lhs, weights):
        total = jnp.zeros((every, TILE), jnp.float32)
        queue = list(turns[SLOT[m] * nh + j])
        for b in queue:
            if SLOT[m] == 0:
                load_up(b).wait()
        for f in range(nf):
            for b in queue[f * len(queue) // nf:(f + 1) * len(queue) // nf]:
                wb[b] = wa[b].T
            total += jnp.dot(
                lhs[:, f * TILE:(f + 1) * TILE], weights[j * nf + f], preferred_element_type=jnp.float32
            )[0:every]
        part[m, j] = total
        moves[m][j].start()

    arrange(0, gx, xs)
    for j in range(nh):
        forward(0, j, xs, wb)
    for b in range(blocks):
        if b not in sum(turns[:nh], []):
            load_up(b).wait()
    for j in range(nh):
        forward(1, j, xs, wa)
    arrange(1, gy, ys)
    for j in range(nh):
        forward(2, j, ys, dt)

    def derive(j):
        for m in range(3):
            moves[m][j].wait_recv()
        gated = part[0, j] + peer[0, j]
        upward = part[1, j] + peer[1, j]
        backward = part[2, j] + peer[2, j]
        sigma = 1.0 / (1.0 + jnp.exp(-gated))
        cols = slice(j * TILE, (j + 1) * TILE)
        dg[0:every, cols] = (backward * upward * sigma * (1.0 + gated * (1.0 - sigma))).astype(jnp.bfloat16)
        du[0:every, cols] = (backward * gated * sigma).astype(jnp.bfloat16)

    def product(f, lo, hi):
        total = jnp.zeros((every, TILE), jnp.float32)
        for j in range(lo, hi):
            cols = slice(j * TILE, (j + 1) * TILE)
            b = j * nf + f
            total += jnp.dot(dg[:, cols], gt[b], preferred_element_type=jnp.float32)[0:every]
            total += jnp.dot(du[:, cols], wb[b], preferred_element_type=jnp.float32)[0:every]
        return total

    sums = [
        [
            remote(
                s0.at[n, p_index(dp), lax.rem(z + dz, nz)], r0.at[n, i],
                r_send.at[n, i], r_recv.at[n, i], device(dz, dp),
            )
            for i, (dz, dp) in enumerate(hops)
        ]
        for n in range(CHUNKS)
    ]

    def send(n):
        at = slice(n * width, (n + 1) * width)
        for q in range(4):
            for k in range(nz):
                top = q * rows + k * tokens
                s0[n, q, k] = acc[top:top + tokens, at].astype(jnp.bfloat16)
        for copy in sums[n]:
            copy.start()

    def store(n):
        at = slice(n * width, (n + 1) * width)
        total = s0[n, plane, z].astype(jnp.float32)
        for i in range(len(hops)):
            sums[n][i].wait_recv()
            total = total + r0[n, i].astype(jnp.float32)
        out_ref[:, at] = gx[plane, z, :, at].astype(jnp.float32) * total

    def columns(f):
        return slice(f * TILE, (f + 1) * TILE)

    for j in range(nh - 1):
        derive(j)
    for f in range(per):
        acc[:, columns(f)] = product(f, 0, nh - 1)
    derive(nh - 1)
    for f in range(per):
        acc[:, columns(f)] += product(f, nh - 1, nh)
    send(0)
    for n in range(1, CHUNKS):
        for f in range(n * per, (n + 1) * per):
            acc[:, columns(f)] = product(f, 0, nh)
        send(n)
    for n in range(CHUNKS):
        store(n)

    for copies in z_copies + p_copies[0] + p_copies[1] + moves + sums:
        for copy in copies:
            copy.wait_send()


def shared(nz, inputs, out_grads, w_gate, w_up, w_down):
    tokens, feats = inputs.shape
    half = w_gate.shape[1] // 2
    nh = half // TILE
    nf = feats // TILE
    width = feats // CHUNKS
    rows = nz * tokens
    every = 4 * rows
    others = 4 * nz - 1
    f32, bf16 = jnp.float32, jnp.bfloat16
    dma = pltpu.SemaphoreType.DMA
    return pl.pallas_call(
        functools.partial(kernel, nz, nf, nh),
        out_shape=jax.ShapeDtypeStruct((tokens, feats), f32),
        in_specs=[pl.BlockSpec(memory_space=pl.ANY)] * 5,
        out_specs=pl.BlockSpec(memory_space=pltpu.VMEM),
        scratch_shapes=[
            pltpu.VMEM((nf * nh, TILE, TILE), bf16),
            pltpu.VMEM((nf * nh, TILE, TILE), bf16),
            pltpu.VMEM((nf * nh, TILE, TILE), bf16),
            pltpu.VMEM((nf * nh, TILE, TILE), bf16),
            pltpu.VMEM((4, nz, tokens, feats), bf16),
            pltpu.VMEM((4, nz, tokens, feats), bf16),
            pltpu.VMEM((every, feats), f32),
            pltpu.VMEM((PADDED, feats), bf16),
            pltpu.VMEM((PADDED, feats), bf16),
            pltpu.VMEM((3, nh, every, TILE), f32),
            pltpu.VMEM((3, nh, every, TILE), f32),
            pltpu.VMEM((PADDED, half), bf16),
            pltpu.VMEM((PADDED, half), bf16),
            pltpu.VMEM((every, feats), f32),
            pltpu.VMEM((CHUNKS, 4, nz, tokens, width), bf16),
            pltpu.VMEM((CHUNKS, others, tokens, width), bf16),
            dma((3, nf * nh)), dma((2,)),
            dma((2, nz - 1)), dma((2, nz - 1)),
            dma((2, nz, 3)), dma((2, nz, 3)),
            dma((3, nh)), dma((3, nh)),
            dma((CHUNKS, others)), dma((CHUNKS, others)),
        ],
        compiler_params=pltpu.CompilerParams(
            collective_id=0, has_side_effects=True, vmem_limit_bytes=60 << 20
        ),
    )(inputs, out_grads, w_gate, w_up, w_down)


def solution(mesh):
    in_specs = (
        P(("groups", "row"), "col"),
        P(("groups", "row"), "col"),
        P("col", "row"),
        P("col", "row"),
        P("row", "col"),
    )
    out_specs = P(("groups", "row"), "col")
    groups, row, col = (mesh.shape[name] for name in ("groups", "row", "col"))

    def body(inputs, out_grads, w_gate, w_up, w_down):
        tokens, feats = inputs.shape
        nz = row // 2
        hidden = w_gate.shape[1]
        held = 4 * feats * hidden + 70 * groups * row * tokens * feats
        fits = (
            groups == 2 and col == 2 and row % 2 == 0 and nz > 1
            and hidden % (2 * TILE) == 0 and feats % (TILE * CHUNKS) == 0 and hidden > 2 * TILE
            and nz * tokens == 8 and held < (58 << 20)
        )
        plan = functools.partial(shared, nz) if fits else per_device
        return plan(inputs, out_grads, w_gate, w_up, w_down)

    return jax.shard_map(
        body, mesh=mesh, in_specs=in_specs, out_specs=out_specs, check_vma=False
    )
```

```python
import functools

import jax
import jax.numpy as jnp
from jax import lax
from jax.experimental import pallas as pl
from jax.experimental.pallas import tpu as pltpu
from jax.sharding import PartitionSpec as P

MESH = pl.DeviceIdType.MESH
TILE = 512
CHUNKS = 2
PADDED = 128
FIRST, STEP, SECOND, THIRD = 8, 2, 20, 8
SLOT = (0, 1, 2)
NT = (((1,), (1,)), ((), ()))


def derivatives(sums):
    gated = sums[0]
    upward = sums[1]
    backward = sums[2]
    sigma = jax.nn.sigmoid(gated)
    grad_gate = (backward * upward * sigma * (1.0 + gated * (1.0 - sigma))).astype(jnp.bfloat16)
    grad_up = (backward * gated * sigma).astype(jnp.bfloat16)
    return jnp.stack([grad_gate, grad_up])


def per_device(inputs, out_grads, w_gate, w_up, w_down):
    stacked = jnp.stack([inputs, out_grads])
    piece = lax.all_gather(stacked, "row", axis=1, tiled=True)
    gated = jnp.dot(piece[0], w_gate, preferred_element_type=jnp.float32)
    upward = jnp.dot(piece[0], w_up, preferred_element_type=jnp.float32)
    backward = lax.dot_general(piece[1], w_down, NT, preferred_element_type=jnp.float32)
    partial_sums = jnp.stack([gated, upward, backward])
    summed = lax.psum(partial_sums, "col")
    derived = derivatives(summed)
    total = lax.dot_general(derived[0], w_gate, NT, preferred_element_type=jnp.float32)
    grad_input = lax.psum_scatter(
        total + lax.dot_general(derived[1], w_up, NT, preferred_element_type=jnp.float32),
        "row",
        scatter_dimension=0,
        tiled=True,
    )
    return inputs.astype(jnp.float32) * grad_input


def kernel(
    nz, nf, nh,
    in_hbm, og_hbm, wg_hbm, wu_hbm, wd_hbm, out_ref,
    wa, wb, dt, gt, gx, gy, stage, xs, ys, part, peer, dg, du, acc, s0, r0,
    w_sem, l_sem, z_send, z_recv, p_send, p_recv, c_send, c_recv, r_send, r_recv,
):
    tokens, feats = in_hbm.shape
    rows = nz * tokens
    every = 4 * rows
    half = nh * TILE
    blocks = nf * nh
    width = feats // CHUNKS
    per = width // TILE
    g = lax.axis_index("groups")
    r = lax.axis_index("row")
    c = lax.axis_index("col")
    x = lax.rem(r, 2)
    z = r // 2
    plane = g * 2 + x

    def p_index(d):
        return lax.rem(plane + d, 4)

    def device(dz, dp):
        q = lax.rem(plane + dp, 4)
        return {"groups": q // 2, "row": lax.rem(z + dz, nz) * 2 + lax.rem(q, 2)}

    hops = [(dz, dp) for dz in (2, 1, 3, 0) for dp in range(4)]
    hops = [(dz, dp) for dz, dp in hops if dz < nz and (dz or dp)]
    hops += [(dz, dp) for dz in range(4, nz) for dp in range(4)]

    def remote(src, dst, send, recv, to):
        return pltpu.make_async_remote_copy(
            src_ref=src, dst_ref=dst, send_sem=send, recv_sem=recv,
            device_id=to, device_id_type=MESH,
        )

    def hid(b):
        return pl.ds(pl.multiple_of(g * half + (b // nf) * TILE, TILE), TILE)

    def fea(b):
        return pl.ds(pl.multiple_of(lax.rem(b, nf) * TILE, TILE), TILE)

    def load_down(b):
        return pltpu.make_async_copy(wd_hbm.at[hid(b), fea(b)], wa.at[b], w_sem.at[0, b])

    def load_gate(b):
        return pltpu.make_async_copy(wg_hbm.at[fea(b), hid(b)], wb.at[b], w_sem.at[1, b])

    def load_up(b):
        return pltpu.make_async_copy(wu_hbm.at[fea(b), hid(b)], wa.at[b], w_sem.at[2, b])

    own = [
        pltpu.make_async_copy(in_hbm, gx.at[plane, z], l_sem.at[0]),
        pltpu.make_async_copy(og_hbm, gy.at[plane, z], l_sem.at[1]),
    ]
    for copy in own:
        copy.start()

    barrier = pltpu.get_barrier_semaphore()
    for dz, dp in [h for h in hops if 0 in h]:
        pl.semaphore_signal(barrier, inc=1, device_id=device(dz, dp), device_id_type=MESH)
    pl.semaphore_signal(barrier, inc=1, device_id={"col": 1 - c}, device_id_type=MESH)

    @pl.loop(0, blocks)
    def _(b):
        load_down(b).start()

    @pl.loop(0, blocks)
    def _(b):
        load_gate(b).start()

    xs[...] = jnp.zeros_like(xs)
    ys[...] = jnp.zeros_like(ys)
    dg[...] = jnp.zeros_like(dg)
    du[...] = jnp.zeros_like(du)

    def turn_down(b):
        load_down(b).wait()
        dt[b] = wa[b].T
        load_up(b).start()

    for copy in own:
        copy.wait()

    def turn_gate(b):
        load_gate(b).wait()
        gt[b] = wb[b].T

    def turn(lo, hi):
        lo, hi = lax.min(lo, 2 * blocks), lax.min(hi, 2 * blocks)
        pl.loop(lax.min(lo, blocks), lax.min(hi, blocks))(turn_down)
        pl.loop(lax.max(lo - blocks, 0), lax.max(hi - blocks, 0))(turn_gate)

    early = lax.max(FIRST - z * STEP, 0)
    turn(jnp.int32(0), early)

    pl.semaphore_wait(barrier, nz + 3)

    buffers = (gx, gy)

    def source(k):
        if k == 0:
            return z
        return jnp.where(z >= k, z - k, k)

    z_copies = [
        [
            remote(buf.at[plane, z], buf.at[plane, z], z_send.at[a, d - 1], z_recv.at[a, d - 1], device(d, 0))
            for d in range(1, nz)
        ]
        for a, buf in enumerate(buffers)
    ]
    p_copies = []
    for a, buf in enumerate(buffers):
        p_copies.append([])
        for k in range(nz):
            block = buf.at[plane, source(k)]
            p_copies[a].append([
                remote(block, block, p_send.at[a, k, d - 1], p_recv.at[a, k, d - 1], device(0, d))
                for d in range(1, 4)
            ])

    def relay(a):
        for k in range(1, nz):
            shift = lax.rem(z + nz - source(k), nz)
            remote(
                buffers[a].at[plane, source(k)], buffers[a].at[plane, source(k)],
                z_send.at[a, shift - 1], z_recv.at[a, shift - 1], device(1, 0),
            ).wait_recv()
            for copy in p_copies[a][k]:
                copy.start()

    for copy in z_copies[0] + p_copies[0][0] + z_copies[1]:
        copy.start()

    turn(early, early + SECOND)
    relay(0)
    turn(early + SECOND, early + SECOND + THIRD)
    for copy in p_copies[1][0]:
        copy.start()
    relay(1)
    turn(early + SECOND + THIRD, jnp.int32(2 * blocks))

    def arrange(a, buf, dst):
        for copies in p_copies[a]:
            for copy in copies:
                copy.wait_recv()
        for q in range(4):
            for k in range(nz):
                at = q * rows + k * tokens
                stage[at:at + tokens, :] = buf[q, k].astype(jnp.float32)
        dst[0:every, :] = stage[...].astype(jnp.bfloat16)

    other = {"col": 1 - c}
    moves = [
        [remote(part.at[m, j], peer.at[m, j], c_send.at[m, j], c_recv.at[m, j], other) for j in range(nh)]
        for m in range(3)
    ]

    turns = [[] for _ in range(3 * nh)]
    slots = 3 * nh - 1
    for b in range(blocks):
        turns[max(1 + b * slots // blocks, b // nf + 1)].append(b)

    def forward(m, j, lhs, weights):
        total = jnp.zeros((every, TILE), jnp.float32)
        queue = list(turns[SLOT[m] * nh + j])
        for b in queue:
            if SLOT[m] == 0:
                load_up(b).wait()
        for f in range(nf):
            for b in queue[f * len(queue) // nf:(f + 1) * len(queue) // nf]:
                wb[b] = wa[b].T
            total += jnp.dot(
                lhs[:, f * TILE:(f + 1) * TILE], weights[j * nf + f], preferred_element_type=jnp.float32
            )[0:every]
        part[m, j] = total
        moves[m][j].start()

    arrange(0, gx, xs)
    for j in range(nh):
        forward(0, j, xs, wb)
    for b in range(blocks):
        if b not in sum(turns[:nh], []):
            load_up(b).wait()
    for j in range(nh):
        forward(1, j, xs, wa)
    arrange(1, gy, ys)
    for j in range(nh):
        forward(2, j, ys, dt)

    def derive(j):
        for m in range(3):
            moves[m][j].wait_recv()
        gated = part[0, j] + peer[0, j]
        upward = part[1, j] + peer[1, j]
        backward = part[2, j] + peer[2, j]
        sigma = 1.0 / (1.0 + jnp.exp(-gated))
        cols = slice(j * TILE, (j + 1) * TILE)
        dg[0:every, cols] = (backward * upward * sigma * (1.0 + gated * (1.0 - sigma))).astype(jnp.bfloat16)
        du[0:every, cols] = (backward * gated * sigma).astype(jnp.bfloat16)

    def product(f, lo, hi):
        total = jnp.zeros((every, TILE), jnp.float32)
        for j in range(lo, hi):
            cols = slice(j * TILE, (j + 1) * TILE)
            b = j * nf + f
            total += jnp.dot(dg[:, cols], gt[b], preferred_element_type=jnp.float32)[0:every]
            total += jnp.dot(du[:, cols], wb[b], preferred_element_type=jnp.float32)[0:every]
        return total

    sums = [
        [
            remote(
                s0.at[n, p_index(dp), lax.rem(z + dz, nz)], r0.at[n, i],
                r_send.at[n, i], r_recv.at[n, i], device(dz, dp),
            )
            for i, (dz, dp) in enumerate(hops)
        ]
        for n in range(CHUNKS)
    ]

    def send(n):
        at = slice(n * width, (n + 1) * width)
        for q in range(4):
            for k in range(nz):
                top = q * rows + k * tokens
                s0[n, q, k] = acc[top:top + tokens, at].astype(jnp.bfloat16)
        for copy in sums[n]:
            copy.start()

    def store(n):
        at = slice(n * width, (n + 1) * width)
        total = s0[n, plane, z].astype(jnp.float32)
        for i in range(len(hops)):
            sums[n][i].wait_recv()
            total = total + r0[n, i].astype(jnp.float32)
        out_ref[:, at] = gx[plane, z, :, at].astype(jnp.float32) * total

    def columns(f):
        return slice(f * TILE, (f + 1) * TILE)

    for j in range(nh - 1):
        derive(j)
    for f in range(per):
        acc[:, columns(f)] = product(f, 0, nh - 1)
    derive(nh - 1)
    for f in range(per):
        acc[:, columns(f)] += product(f, nh - 1, nh)
    send(0)
    for n in range(1, CHUNKS):
        for f in range(n * per, (n + 1) * per):
            acc[:, columns(f)] = product(f, 0, nh)
        send(n)
    for n in range(CHUNKS):
        store(n)

    for copies in z_copies + p_copies[0] + p_copies[1] + moves + sums:
        for copy in copies:
            copy.wait_send()


def shared(nz, inputs, out_grads, w_gate, w_up, w_down):
    tokens, feats = inputs.shape
    half = w_gate.shape[1] // 2
    nh = half // TILE
    nf = feats // TILE
    width = feats // CHUNKS
    rows = nz * tokens
    every = 4 * rows
    others = 4 * nz - 1
    f32, bf16 = jnp.float32, jnp.bfloat16
    dma = pltpu.SemaphoreType.DMA
    return pl.pallas_call(
        functools.partial(kernel, nz, nf, nh),
        out_shape=pltpu.VMEM((tokens, feats), f32),
        in_specs=[pl.BlockSpec(memory_space=pl.ANY)] * 5,
        out_specs=pl.BlockSpec(memory_space=pltpu.VMEM),
        scratch_shapes=[
            pltpu.VMEM((nf * nh, TILE, TILE), bf16),
            pltpu.VMEM((nf * nh, TILE, TILE), bf16),
            pltpu.VMEM((nf * nh, TILE, TILE), bf16),
            pltpu.VMEM((nf * nh, TILE, TILE), bf16),
            pltpu.VMEM((4, nz, tokens, feats), bf16),
            pltpu.VMEM((4, nz, tokens, feats), bf16),
            pltpu.VMEM((every, feats), f32),
            pltpu.VMEM((PADDED, feats), bf16),
            pltpu.VMEM((PADDED, feats), bf16),
            pltpu.VMEM((3, nh, every, TILE), f32),
            pltpu.VMEM((3, nh, every, TILE), f32),
            pltpu.VMEM((PADDED, half), bf16),
            pltpu.VMEM((PADDED, half), bf16),
            pltpu.VMEM((every, feats), f32),
            pltpu.VMEM((CHUNKS, 4, nz, tokens, width), bf16),
            pltpu.VMEM((CHUNKS, others, tokens, width), bf16),
            dma((3, nf * nh)), dma((2,)),
            dma((2, nz - 1)), dma((2, nz - 1)),
            dma((2, nz, 3)), dma((2, nz, 3)),
            dma((3, nh)), dma((3, nh)),
            dma((CHUNKS, others)), dma((CHUNKS, others)),
        ],
        compiler_params=pltpu.CompilerParams(
            collective_id=0, has_side_effects=True, vmem_limit_bytes=60 << 20
        ),
    )(inputs, out_grads, w_gate, w_up, w_down)


def solution(mesh):
    in_specs = (
        P(("groups", "row"), "col"),
        P(("groups", "row"), "col"),
        P("col", "row"),
        P("col", "row"),
        P("row", "col"),
    )
    out_specs = P(("groups", "row"), "col")
    groups, row, col = (mesh.shape[name] for name in ("groups", "row", "col"))

    def body(inputs, out_grads, w_gate, w_up, w_down):
        tokens, feats = inputs.shape
        nz = row // 2
        hidden = w_gate.shape[1]
        held = 4 * feats * hidden + 70 * groups * row * tokens * feats
        fits = (
            groups == 2 and col == 2 and row % 2 == 0 and nz > 1
            and hidden % (2 * TILE) == 0 and feats % (TILE * CHUNKS) == 0 and hidden > 2 * TILE
            and nz * tokens == 8 and held < (58 << 20)
        )
        plan = functools.partial(shared, nz) if fits else per_device
        return plan(inputs, out_grads, w_gate, w_up, w_down)

    return jax.shard_map(
        body, mesh=mesh, in_specs=in_specs, out_specs=out_specs, check_vma=False
    )
```

```python
import functools

import jax
import jax.numpy as jnp
from jax import lax
from jax.experimental import pallas as pl
from jax.experimental.pallas import tpu as pltpu
from jax.sharding import PartitionSpec as P

MESH = pl.DeviceIdType.MESH
TILE = 512
CHUNKS = 2
PADDED = 128
FIRST, STEP, SECOND, THIRD = 8, 2, 20, 8
SLOT = (0, 1, 2)
NT = (((1,), (1,)), ((), ()))


def derivatives(sums):
    gated = sums[0]
    upward = sums[1]
    backward = sums[2]
    sigma = jax.nn.sigmoid(gated)
    grad_gate = (backward * upward * sigma * (1.0 + gated * (1.0 - sigma))).astype(jnp.bfloat16)
    grad_up = (backward * gated * sigma).astype(jnp.bfloat16)
    return jnp.stack([grad_gate, grad_up])


def per_device(inputs, out_grads, w_gate, w_up, w_down):
    stacked = jnp.stack([inputs, out_grads])
    piece = lax.all_gather(stacked, "row", axis=1, tiled=True)
    gated = jnp.dot(piece[0], w_gate, preferred_element_type=jnp.float32)
    upward = jnp.dot(piece[0], w_up, preferred_element_type=jnp.float32)
    backward = lax.dot_general(piece[1], w_down, NT, preferred_element_type=jnp.float32)
    partial_sums = jnp.stack([gated, upward, backward])
    summed = lax.psum(partial_sums, "col")
    derived = derivatives(summed)
    total = lax.dot_general(derived[0], w_gate, NT, preferred_element_type=jnp.float32)
    grad_input = lax.psum_scatter(
        total + lax.dot_general(derived[1], w_up, NT, preferred_element_type=jnp.float32),
        "row",
        scatter_dimension=0,
        tiled=True,
    )
    return inputs.astype(jnp.float32) * grad_input


def kernel(
    nz, nf, nh,
    in_hbm, og_hbm, wg_hbm, wu_hbm, wd_hbm, out_ref,
    wa, wb, dt, gt, gx, gy, stage, xs, ys, part, peer, dg, du, acc, s0, r0,
    w_sem, l_sem, z_send, z_recv, p_send, p_recv, c_send, c_recv, r_send, r_recv,
):
    tokens, feats = in_hbm.shape
    rows = nz * tokens
    every = 4 * rows
    half = nh * TILE
    blocks = nf * nh
    width = feats // CHUNKS
    per = width // TILE
    g = lax.axis_index("groups")
    r = lax.axis_index("row")
    c = lax.axis_index("col")
    x = lax.rem(r, 2)
    z = r // 2
    plane = g * 2 + x

    def p_index(d):
        return lax.rem(plane + d, 4)

    def device(dz, dp):
        q = lax.rem(plane + dp, 4)
        return {"groups": q // 2, "row": lax.rem(z + dz, nz) * 2 + lax.rem(q, 2)}

    hops = [(dz, dp) for dz in (2, 1, 3, 0) for dp in range(4)]
    hops = [(dz, dp) for dz, dp in hops if dz < nz and (dz or dp)]
    hops += [(dz, dp) for dz in range(4, nz) for dp in range(4)]

    def remote(src, dst, send, recv, to):
        return pltpu.make_async_remote_copy(
            src_ref=src, dst_ref=dst, send_sem=send, recv_sem=recv,
            device_id=to, device_id_type=MESH,
        )

    def hid(b):
        return pl.ds(pl.multiple_of(g * half + (b // nf) * TILE, TILE), TILE)

    def fea(b):
        return pl.ds(pl.multiple_of(lax.rem(b, nf) * TILE, TILE), TILE)

    def load_down(b):
        return pltpu.make_async_copy(wd_hbm.at[hid(b), fea(b)], wa.at[b], w_sem.at[0, b])

    def load_gate(b):
        return pltpu.make_async_copy(wg_hbm.at[fea(b), hid(b)], wb.at[b], w_sem.at[1, b])

    def load_up(b):
        return pltpu.make_async_copy(wu_hbm.at[fea(b), hid(b)], wa.at[b], w_sem.at[2, b])

    own = [
        pltpu.make_async_copy(in_hbm, gx.at[plane, z], l_sem.at[0]),
        pltpu.make_async_copy(og_hbm, gy.at[plane, z], l_sem.at[1]),
    ]
    for copy in own:
        copy.start()

    barrier = pltpu.get_barrier_semaphore()
    for dz, dp in [h for h in hops if 0 in h]:
        pl.semaphore_signal(barrier, inc=1, device_id=device(dz, dp), device_id_type=MESH)
    pl.semaphore_signal(barrier, inc=1, device_id={"col": 1 - c}, device_id_type=MESH)

    @pl.loop(0, blocks)
    def _(b):
        load_down(b).start()

    @pl.loop(0, blocks)
    def _(b):
        load_gate(b).start()

    xs[...] = jnp.zeros_like(xs)
    ys[...] = jnp.zeros_like(ys)
    dg[...] = jnp.zeros_like(dg)
    du[...] = jnp.zeros_like(du)

    def turn_down(b):
        load_down(b).wait()
        dt[b] = wa[b].T
        load_up(b).start()

    for copy in own:
        copy.wait()

    def turn_gate(b):
        load_gate(b).wait()
        gt[b] = wb[b].T

    def turn(lo, hi):
        lo, hi = lax.min(lo, 2 * blocks), lax.min(hi, 2 * blocks)
        pl.loop(lax.min(lo, blocks), lax.min(hi, blocks))(turn_down)
        pl.loop(lax.max(lo - blocks, 0), lax.max(hi - blocks, 0))(turn_gate)

    early = lax.max(FIRST - z * STEP, 0)
    turn(jnp.int32(0), early)

    pl.semaphore_wait(barrier, nz + 3)

    buffers = (gx, gy)

    def source(k):
        if k == 0:
            return z
        return jnp.where(z >= k, z - k, k)

    z_copies = [
        [
            remote(buf.at[plane, z], buf.at[plane, z], z_send.at[a, d - 1], z_recv.at[a, d - 1], device(d, 0))
            for d in range(1, nz)
        ]
        for a, buf in enumerate(buffers)
    ]
    p_copies = []
    for a, buf in enumerate(buffers):
        p_copies.append([])
        for k in range(nz):
            block = buf.at[plane, source(k)]
            p_copies[a].append([
                remote(block, block, p_send.at[a, k, d - 1], p_recv.at[a, k, d - 1], device(0, d))
                for d in range(1, 4)
            ])

    def relay(a):
        for k in range(1, nz):
            shift = lax.rem(z + nz - source(k), nz)
            remote(
                buffers[a].at[plane, source(k)], buffers[a].at[plane, source(k)],
                z_send.at[a, shift - 1], z_recv.at[a, shift - 1], device(1, 0),
            ).wait_recv()
            for copy in p_copies[a][k]:
                copy.start()

    for copy in z_copies[0] + p_copies[0][0] + z_copies[1]:
        copy.start()

    turn(early, early + SECOND)
    relay(0)
    turn(early + SECOND, early + SECOND + THIRD)
    for copy in p_copies[1][0]:
        copy.start()
    relay(1)
    turn(early + SECOND + THIRD, jnp.int32(2 * blocks))

    def arrange(a, buf, dst):
        for copies in p_copies[a]:
            for copy in copies:
                copy.wait_recv()
        dst[0:every, :] = buf[...].reshape(every, feats)

    other = {"col": 1 - c}
    moves = [
        [remote(part.at[m, j], peer.at[m, j], c_send.at[m, j], c_recv.at[m, j], other) for j in range(nh)]
        for m in range(3)
    ]

    turns = [[] for _ in range(3 * nh)]
    slots = 3 * nh - 1
    for b in range(blocks):
        turns[max(1 + b * slots // blocks, b // nf + 1)].append(b)

    def forward(m, j, lhs, weights):
        total = jnp.zeros((every, TILE), jnp.float32)
        queue = list(turns[SLOT[m] * nh + j])
        for b in queue:
            if SLOT[m] == 0:
                load_up(b).wait()
        for f in range(nf):
            for b in queue[f * len(queue) // nf:(f + 1) * len(queue) // nf]:
                wb[b] = wa[b].T
            total += jnp.dot(
                lhs[:, f * TILE:(f + 1) * TILE], weights[j * nf + f], preferred_element_type=jnp.float32
            )[0:every]
        part[m, j] = total
        moves[m][j].start()

    arrange(0, gx, xs)
    for j in range(nh):
        forward(0, j, xs, wb)
    for b in range(blocks):
        if b not in sum(turns[:nh], []):
            load_up(b).wait()
    for j in range(nh):
        forward(1, j, xs, wa)
    arrange(1, gy, ys)
    for j in range(nh):
        forward(2, j, ys, dt)

    def derive(j):
        for m in range(3):
            moves[m][j].wait_recv()
        gated = part[0, j] + peer[0, j]
        upward = part[1, j] + peer[1, j]
        backward = part[2, j] + peer[2, j]
        sigma = 1.0 / (1.0 + jnp.exp(-gated))
        cols = slice(j * TILE, (j + 1) * TILE)
        dg[0:every, cols] = (backward * upward * sigma * (1.0 + gated * (1.0 - sigma))).astype(jnp.bfloat16)
        du[0:every, cols] = (backward * gated * sigma).astype(jnp.bfloat16)

    def product(f, lo, hi):
        total = jnp.zeros((every, TILE), jnp.float32)
        for j in range(lo, hi):
            cols = slice(j * TILE, (j + 1) * TILE)
            b = j * nf + f
            total += jnp.dot(dg[:, cols], gt[b], preferred_element_type=jnp.float32)[0:every]
            total += jnp.dot(du[:, cols], wb[b], preferred_element_type=jnp.float32)[0:every]
        return total

    me = z * 4 + plane

    def passing(n, i):
        t = jnp.where(i >= me, i + 1, i)
        slot = jnp.where(me > t, me - 1, me)
        q = lax.rem(t, 4)
        return remote(
            s0.at[n, q, t // 4], r0.at[n, slot], r_send.at[n, i], r_recv.at[n, slot],
            {"groups": q // 2, "row": t // 4 * 2 + lax.rem(q, 2)},
        )

    def landing(n, i):
        return remote(
            s0.at[n, 0, 0], r0.at[n, i], r_send.at[n, i], r_recv.at[n, i], device(1, 0)
        )

    sums = [[passing(n, i) for i in range(len(hops))] for n in range(CHUNKS)]

    def send(n):
        at = slice(n * width, (n + 1) * width)
        for q in range(4):
            for k in range(nz):
                top = q * rows + k * tokens
                s0[n, q, k] = acc[top:top + tokens, at].astype(jnp.bfloat16)
        for copy in sums[n]:
            copy.start()

    def store(n):
        at = slice(n * width, (n + 1) * width)
        total = s0[n, plane, z].astype(jnp.float32)
        for i in range(len(hops)):
            landing(n, i).wait_recv()
            total = total + r0[n, i].astype(jnp.float32)
        out_ref[:, at] = gx[plane, z, :, at].astype(jnp.float32) * total

    def columns(f):
        return slice(f * TILE, (f + 1) * TILE)

    for j in range(nh - 1):
        derive(j)
    for f in range(per):
        acc[:, columns(f)] = product(f, 0, nh - 1)
    derive(nh - 1)
    for f in range(per):
        acc[:, columns(f)] += product(f, nh - 1, nh)
    send(0)
    for n in range(1, CHUNKS):
        for f in range(n * per, (n + 1) * per):
            acc[:, columns(f)] = product(f, 0, nh)
        send(n)
    for n in range(CHUNKS):
        store(n)

    for copies in z_copies + p_copies[0] + p_copies[1] + moves + sums:
        for copy in copies:
            copy.wait_send()


def shared(nz, inputs, out_grads, w_gate, w_up, w_down):
    tokens, feats = inputs.shape
    half = w_gate.shape[1] // 2
    nh = half // TILE
    nf = feats // TILE
    width = feats // CHUNKS
    rows = nz * tokens
    every = 4 * rows
    others = 4 * nz - 1
    f32, bf16 = jnp.float32, jnp.bfloat16
    dma = pltpu.SemaphoreType.DMA
    return pl.pallas_call(
        functools.partial(kernel, nz, nf, nh),
        out_shape=pltpu.VMEM((tokens, feats), f32),
        in_specs=[pl.BlockSpec(memory_space=pl.ANY)] * 5,
        out_specs=pl.BlockSpec(memory_space=pltpu.VMEM),
        scratch_shapes=[
            pltpu.VMEM((nf * nh, TILE, TILE), bf16),
            pltpu.VMEM((nf * nh, TILE, TILE), bf16),
            pltpu.VMEM((nf * nh, TILE, TILE), bf16),
            pltpu.VMEM((nf * nh, TILE, TILE), bf16),
            pltpu.VMEM((4, nz, tokens, feats), bf16),
            pltpu.VMEM((4, nz, tokens, feats), bf16),
            pltpu.VMEM((every, feats), f32),
            pltpu.VMEM((PADDED, feats), bf16),
            pltpu.VMEM((PADDED, feats), bf16),
            pltpu.VMEM((3, nh, every, TILE), f32),
            pltpu.VMEM((3, nh, every, TILE), f32),
            pltpu.VMEM((PADDED, half), bf16),
            pltpu.VMEM((PADDED, half), bf16),
            pltpu.VMEM((every, feats), f32),
            pltpu.VMEM((CHUNKS, 4, nz, tokens, width), bf16),
            pltpu.VMEM((CHUNKS, others, tokens, width), bf16),
            dma((3, nf * nh)), dma((2,)),
            dma((2, nz - 1)), dma((2, nz - 1)),
            dma((2, nz, 3)), dma((2, nz, 3)),
            dma((3, nh)), dma((3, nh)),
            dma((CHUNKS, others)), dma((CHUNKS, others)),
        ],
        compiler_params=pltpu.CompilerParams(
            collective_id=0, has_side_effects=True, vmem_limit_bytes=60 << 20
        ),
    )(inputs, out_grads, w_gate, w_up, w_down)


def solution(mesh):
    in_specs = (
        P(("groups", "row"), "col"),
        P(("groups", "row"), "col"),
        P("col", "row"),
        P("col", "row"),
        P("row", "col"),
    )
    out_specs = P(("groups", "row"), "col")
    groups, row, col = (mesh.shape[name] for name in ("groups", "row", "col"))

    def body(inputs, out_grads, w_gate, w_up, w_down):
        tokens, feats = inputs.shape
        nz = row // 2
        hidden = w_gate.shape[1]
        held = 4 * feats * hidden + 70 * groups * row * tokens * feats
        fits = (
            groups == 2 and col == 2 and row % 2 == 0 and nz > 1
            and hidden % (2 * TILE) == 0 and feats % (TILE * CHUNKS) == 0 and hidden > 2 * TILE
            and nz * tokens == 8 and held < (58 << 20)
        )
        plan = functools.partial(shared, nz) if fits else per_device
        return plan(inputs, out_grads, w_gate, w_up, w_down)

    return jax.shard_map(
        body, mesh=mesh, in_specs=in_specs, out_specs=out_specs, check_vma=False
    )
```
